32 devices in a mesh: cfg: 2 (over y), req: 4 (over x, core), seq: 4 (over z).
Axes of the slice: x: 2, y: 2, z: 4, core: 2. Of those that a mesh axis runs over, the one named last changes fastest.
Arguments:
- image_hidden: bfloat16 [2, 4, 512, 1536], P('cfg', 'req', 'seq'), may hold values from -6 to 6
- text_hidden: bfloat16 [2, 4, 160, 1536], P('cfg', 'req', 'seq'), may hold values from -6 to 6
- modulation: float32 [2, 4, 10, 1536], P('cfg', 'req'), may hold values from -3 to 3
- attn_weight: bfloat16 [1536, 5120], P(None, 'seq'), may hold values from -8 to 8
- proj_weight: bfloat16 [1024, 1536], replicated, may hold values from -0.1875 to 0.1875
- mlp_in_weight: bfloat16 [1536, 6144], P(None, 'seq'), may hold values from -0.15625 to 0.15625
- mlp_out_weight: bfloat16 [6144, 1536], P('seq'), may hold values from -0.078125 to 0.078125
- final_weight: bfloat16 [64, 1536], replicated, may hold values from -0.15625 to 0.15625
- latents: float32 [4, 64, 512], P('req', 'cfg', 'seq'), may hold values from -6 to 6
- guidance: float32 [4], P('req'), may hold values from 3 to 7
- text_lengths: int32 [2, 4], P('cfg', 'req'), may hold values from 1 to 154, 385 in all within a row
- step_index: int32 [4], P('req'), may hold values from 0 to 27
- step_count: int32 [4], P('req'), may hold values from 1 to 3
Outputs:
- velocity: float32 [4, 64, 512], P('req', 'cfg', 'seq')
- new_latents: float32 [4, 64, 512], P('req', 'cfg', 'seq')
The draws below stay inside these ranges and needn't reach their ends.
All inputs are finite; a program needn't handle non-finite values. No bound on the sum of `text_lengths` on one device may be relied on, other than what follows from the above.
Results may differ from the reference program's by a relative error of at most 0.017.
Values may be sent and summed in bfloat16 or wider, within the bound.
A program may use at most 128 MiB of HBM per device.

```python
import math
import jax
import jax.numpy as jnp
import numpy as np
from jax import lax

D = 1536
HEADS = 16
HEAD = 64
FF = 6144
PATCH = 64
TXT = 160
TXT_MAX = 154
STEPS = 28
IMG = 512
REQ = 4
N_SEQ = 4


def draw_attn_weight(key, part):
    base = jnp.clip(jax.random.normal(key, (D, HEADS, 5, HEAD), jnp.float32), -6.0, 6.0) / jnp.sqrt(float(D))
    base = jnp.clip(base, -8.0, 8.0)
    return base.reshape(D, HEADS * 5 * HEAD).astype(jnp.bfloat16)


def draw_image_hidden(key, part):
    first_key = jax.random.fold_in(key, 21)
    second_key = jax.random.fold_in(key, 22)
    ramp = (jnp.arange(IMG, dtype=jnp.float32) + 0.5) / IMG
    shared = jnp.clip(jax.random.normal(first_key, (REQ, IMG, D), jnp.float32), -6.0, 6.0)
    other = jnp.clip(jax.random.normal(second_key, (REQ, IMG, D), jnp.float32), -6.0, 6.0)
    mixing = ramp[None, :, None]
    second = (1.0 - mixing) * shared + mixing * other
    result = jnp.clip(jnp.stack([shared, second], axis=0), -6.0, 6.0)
    return result.astype(jnp.bfloat16)


def draw_modulation(key, part):
    base = 0.5 * jax.random.normal(jax.random.fold_in(key, 31), (REQ, 10, D), jnp.float32)
    offset = 0.1 * jax.random.normal(jax.random.fold_in(key, 32), (REQ, 10, D), jnp.float32)
    result = jnp.stack([base, base + offset], axis=0)
    return jnp.clip(result, -3.0, 3.0).astype(jnp.float32)


def plant(array, own_key, smallest, top_value):
    longest = array.shape.index(max(array.shape))
    spots = []
    for shift in (0, 1):
        where = [jax.random.randint(jax.random.fold_in(own_key, axis), (), 0, length) for axis, length in enumerate(array.shape)]
        where[longest] = (where[longest] + shift) % array.shape[longest]
        spots.append(tuple(where))
    return array.at[spots[0]].set(smallest).at[spots[1]].set(top_value)


def levels(own_key, dims, shards, least, largest):
    gain, own = 1.0, jax.random.fold_in(own_key, 6)
    for axis_at, shards_of in shards:
        heights = jnp.exp(jax.random.uniform(jax.random.fold_in(own, axis_at), (shards_of,), jnp.float32, least / len(shards), largest / len(shards)))
        gain = gain * jnp.repeat(heights, dims[axis_at] // shards_of).reshape([-1 if axis == axis_at else 1 for axis in range(len(dims))])
    return gain


def split_up(number_of, total, most, lean):
    weights = [(1 << 20) // math.isqrt(rank ** lean) + 1 for rank in range(2, number_of + 1)]
    surplus, holding = total - most - (number_of - 1), [1] * (number_of - 1)
    while surplus > 0:
        movable = [i for i in range(number_of - 1) if holding[i] < most]
        whole, budget = sum([weights[i] for i in movable]), surplus
        for i in movable:
            extra = min(most - holding[i], max(1, budget * weights[i] // whole), surplus)
            holding[i] = holding[i] + extra
            surplus = surplus - extra
    return np.array([most] + holding)


def ragged_sizes(stream_key, count, total, most, slope):
    if count == 2:
        one = jax.random.randint(stream_key, (), max(1, total - most), min(most, total - 1) + 1)
        return jnp.stack([one, total - one])
    sizes = jnp.asarray(split_up(count, total, most, slope), jnp.int32)
    twos = (count - 1) // 2
    giver, sink = sizes[1:1 + 2 * twos:2], sizes[2:2 + 2 * twos:2]
    room = jnp.minimum(giver - 1, most - sink)
    passed = jax.random.randint(jax.random.fold_in(stream_key, 1), (twos,), 0, 1 << 20) % (room + 1)
    sizes = sizes.at[1:1 + 2 * twos:2].set(giver - passed).at[2:2 + 2 * twos:2].set(sink + passed)
    return sizes[jax.random.permutation(jax.random.fold_in(stream_key, 2), count)]


def normal_values(rng, shape, scale, reach, shards=(), held_as=jnp.bfloat16):
    level = levels(rng, shape, shards, -0.22, 0.18) if shards else 1.0
    values = jax.random.normal(rng, shape, jnp.float32) * scale * level
    return jnp.minimum(jnp.maximum(values, -reach), reach).astype(held_as)


def setup_inputs(seed: int = 0) -> dict:
    key_list = jax.random.split(jax.random.key(seed), 14)
    image_hidden = draw_image_hidden(jax.random.fold_in(key_list[13], 71), 0)
    text_hidden = normal_values(key_list[1], (2, REQ, TXT, D), 1.0, 6.0, ((0, 2), (1, 4), (2, 4)))
    modulation = draw_modulation(jax.random.fold_in(key_list[13], 71), 0)
    attn_weight = draw_attn_weight(jax.random.fold_in(key_list[13], 71), 0)
    proj_weight = normal_values(key_list[4], (HEADS * HEAD, D), (HEADS * HEAD) ** -0.5, 0.1875)
    mlp_in_weight = normal_values(key_list[5], (D, FF), D ** -0.5, 0.15625, ((1, 4),))
    mlp_out_weight = normal_values(key_list[6], (FF, D), FF ** -0.5, 0.078125, ((0, 4),))
    final_weight = normal_values(key_list[7], (PATCH, D), D ** -0.5, 0.15625)
    latents = normal_values(key_list[8], (REQ, PATCH, IMG), 1.0, 6.0, ((0, 4), (1, 2), (2, 4)), jnp.float32)
    guidance = jnp.clip(3.0 + 4.0 * jax.random.uniform(key_list[9], (REQ,), jnp.float32) ** levels(key_list[9], (REQ,), ((0, 4),), -0.2, 0.2), 3.0, 7.0)
    text_lengths = jax.vmap(lambda own: ragged_sizes(own, REQ, (TXT_MAX // 2) * (REQ + 1), TXT_MAX, 0))(jax.random.split(key_list[10], 2)).reshape((2, REQ)).astype(jnp.int32)
    step_index = plant(jax.random.randint(key_list[11], (REQ,), 0, STEPS), jax.random.fold_in(key_list[11], 1), 0, STEPS - 1).astype(jnp.int32)
    step_count = plant(jax.random.randint(key_list[12], (REQ,), 1, 4), jax.random.fold_in(key_list[12], 1), 1, 3).astype(jnp.int32)
    return dict(image_hidden=image_hidden, text_hidden=text_hidden, modulation=modulation, attn_weight=attn_weight, proj_weight=proj_weight, mlp_in_weight=mlp_in_weight, mlp_out_weight=mlp_out_weight, final_weight=final_weight, latents=latents, guidance=guidance, text_lengths=text_lengths, step_index=step_index, step_count=step_count)


EPS_NORM = 1e-06

def modulate(rows_in, scale_row, shift_row):
    values = rows_in.astype(jnp.float32)
    center = lax.optimization_barrier(jnp.mean(values, axis=-1, keepdims=True))
    spread = lax.optimization_barrier(jnp.mean(jnp.square(values - center), axis=-1, keepdims=True))
    return ((values - center) * lax.rsqrt(spread + EPS_NORM) * (1.0 + scale_row) + shift_row).astype(jnp.bfloat16)

def sigma_of(index):
    remain = 1.0 - index.astype(jnp.float32) / STEPS
    return 3.0 * remain / (1.0 + 2.0 * remain)

def mlp_part(hidden, mod_rows, mlp_in_weight, mlp_out_weight):
    mlp_norm = modulate(hidden, mod_rows[8], mod_rows[7])
    inner = jax.nn.gelu(jnp.dot(mlp_norm, mlp_in_weight, preferred_element_type=jnp.float32), approximate=True).astype(jnp.bfloat16)
    units = FF // N_SEQ
    inner_groups = jnp.transpose(inner.reshape(IMG, N_SEQ, units), (1, 0, 2))
    weight_groups = mlp_out_weight.reshape(N_SEQ, units, D)

    def add_group(carry, items):
        inner_group, weight_group = items
        partial_sum = jnp.dot(inner_group, weight_group, preferred_element_type=jnp.float32).astype(jnp.bfloat16)
        return (carry + partial_sum.astype(jnp.float32), None)
    mlp_out, unused = lax.scan(add_group, jnp.zeros((IMG, D), jnp.float32), (inner_groups, weight_groups))
    return hidden + mod_rows[9] * mlp_out

def branch_velocity(image_rows, text_rows, mod_rows, length, attn_weight, proj_weight, mlp_in_weight, mlp_out_weight, final_weight):
    image_norm = modulate(image_rows, mod_rows[1], mod_rows[0])
    text_norm = modulate(text_rows, mod_rows[4], mod_rows[3])
    split_cols = attn_weight.reshape(D, HEADS, 5, HEAD)
    image_cols = split_cols[:, :, 0:3, :].reshape(D, HEADS * 3 * HEAD)
    text_cols = split_cols[:, :, 3:5, :].reshape(D, HEADS * 2 * HEAD)
    image_qkv = jnp.dot(image_norm, image_cols, preferred_element_type=jnp.float32).astype(jnp.bfloat16)
    image_qkv = image_qkv.reshape(IMG, HEADS, 3, HEAD)
    text_kv = jnp.dot(text_norm, text_cols, preferred_element_type=jnp.float32).astype(jnp.bfloat16)
    text_kv = text_kv.reshape(TXT, HEADS, 2, HEAD)
    keys_all = jnp.concatenate([image_qkv[:, :, 1], text_kv[:, :, 0]], axis=0)
    values_all = jnp.concatenate([image_qkv[:, :, 2], text_kv[:, :, 1]], axis=0)
    slots = jnp.arange(TXT, dtype=jnp.int32)
    valid = jnp.concatenate([jnp.ones((IMG,), dtype=bool), slots < length])
    queries = jnp.transpose(image_qkv[:, :, 0], (1, 0, 2))
    keys_all = jnp.transpose(keys_all, (1, 0, 2))
    values_all = jnp.transpose(values_all, (1, 0, 2))

    def one_head(items):
        query_head, key_head, value_head = items
        scores = jnp.dot(query_head, key_head.T, preferred_element_type=jnp.float32) * HEAD ** (-0.5)
        scores = jnp.where(valid[None, :], scores, -1e+30)
        row_max = lax.optimization_barrier(jnp.max(scores, axis=1, keepdims=True))
        weights = jnp.exp(scores - row_max)
        total = lax.optimization_barrier(jnp.sum(weights, axis=1, keepdims=True))
        probs = weights.astype(jnp.bfloat16)
        return (jnp.dot(probs, value_head, preferred_element_type=jnp.float32) / total).astype(jnp.bfloat16)
    attended = lax.map(one_head, (queries, keys_all, values_all))
    attended = jnp.transpose(attended, (1, 0, 2)).reshape(IMG, HEADS * HEAD)
    hidden = image_rows.astype(jnp.float32) + mod_rows[2] * jnp.dot(attended, proj_weight, preferred_element_type=jnp.float32)
    block_out = mlp_part(hidden, mod_rows, mlp_in_weight, mlp_out_weight)
    final_norm = modulate(block_out, mod_rows[6], mod_rows[5])
    return jnp.dot(final_weight, final_norm.T, preferred_element_type=jnp.float32)

def reference(image_hidden, text_hidden, modulation, attn_weight, proj_weight, mlp_in_weight, mlp_out_weight, final_weight, latents, guidance, text_lengths, step_index, step_count):

    def per_request(items):
        image_pair, text_pair, mod_pair, length_pair, guide_one, latent_one, index_one, count_one = items
        cond_vel = branch_velocity(image_pair[0], text_pair[0], mod_pair[0], length_pair[0], attn_weight, proj_weight, mlp_in_weight, mlp_out_weight, final_weight)
        uncond_vel = branch_velocity(image_pair[1], text_pair[1], mod_pair[1], length_pair[1], attn_weight, proj_weight, mlp_in_weight, mlp_out_weight, final_weight)
        guided = uncond_vel + guide_one * (cond_vel - uncond_vel)
        entries = PATCH * IMG
        rms_cond = jnp.sqrt(jnp.sum(cond_vel * cond_vel) / entries + EPS_NORM)
        rms_guided = jnp.sqrt(jnp.sum(guided * guided) / entries + EPS_NORM)
        result_vel = 0.7 * (guided * (rms_cond / rms_guided)) + 0.3 * guided
        next_index = jnp.minimum(index_one + count_one, STEPS)
        step_size = sigma_of(next_index) - sigma_of(index_one)
        return (result_vel, latent_one + step_size * result_vel)
    velocity, new_latents = lax.map(per_request, (jnp.swapaxes(image_hidden, 0, 1), jnp.swapaxes(text_hidden, 0, 1), jnp.swapaxes(modulation, 0, 1), jnp.swapaxes(text_lengths, 0, 1), guidance, latents, step_index, step_count))
    return (velocity, new_latents)
```

```python
import jax
import jax.numpy as jnp
from jax import lax
from jax.sharding import PartitionSpec as P

HEADS = 16
HEAD = 64
STEPS = 28


EPS_NORM = 1e-06


def partner(value, axis, distance):
    mask = 2**distance
    pairs = [(source, source ^ mask) for source in range(lax.axis_size(axis))]
    return lax.ppermute(value, axis, pairs)


def modulate(rows_in, scale_row, shift_row):
    values = rows_in.astype(jnp.float32)
    center = jnp.mean(values, axis=-1, keepdims=True)
    spread = jnp.mean(jnp.square(values - center), axis=-1, keepdims=True)
    return (
        (values - center) * lax.rsqrt(spread + EPS_NORM) * (1.0 + scale_row) + shift_row
    ).astype(jnp.bfloat16)


def sigma_of(index):
    remain = 1.0 - index.astype(jnp.float32) / STEPS
    return 3.0 * remain / (1.0 + 2.0 * remain)


def split_columns(weight_piece):
    width_in = weight_piece.shape[0]
    head_count = weight_piece.shape[1] // (5 * HEAD)
    shaped = weight_piece.reshape(width_in, head_count, 5, HEAD)
    image_cols = shaped[:, :, 0:3, :].reshape(width_in, head_count * 3 * HEAD)
    text_cols = shaped[:, :, 3:5, :].reshape(width_in, head_count * 2 * HEAD)
    return (image_cols, text_cols)


def local(
    image_hidden,
    text_hidden,
    modulation,
    attn_weight,
    proj_weight,
    mlp_in_weight,
    mlp_out_weight,
    final_weight,
    latents,
    guidance,
    text_lengths,
    step_index,
    step_count,
):
    seq_size = lax.axis_size("seq")
    local_heads = HEADS // seq_size
    image_rows = image_hidden[0, 0]
    text_rows = text_hidden[0, 0]
    mod_rows = modulation[0, 0]
    local_rows = image_rows.shape[0]
    image_total = local_rows * seq_size
    text_total = text_rows.shape[0] * seq_size
    image_norm = modulate(image_rows, mod_rows[1], mod_rows[0])
    text_norm = modulate(text_rows, mod_rows[4], mod_rows[3])
    gathered = lax.all_gather(jnp.concatenate([image_norm, text_norm], axis=0), "seq", axis=0)
    image_all = gathered[:, :local_rows].reshape(image_total, -1)
    text_all = gathered[:, local_rows:].reshape(text_total, -1)
    image_cols, text_cols = split_columns(attn_weight)
    image_qkv = jnp.dot(image_all, image_cols, preferred_element_type=jnp.float32).astype(
        jnp.bfloat16
    )
    text_kv = jnp.dot(text_all, text_cols, preferred_element_type=jnp.float32).astype(
        jnp.bfloat16
    )
    image_qkv = image_qkv.reshape(image_total, local_heads, 3, HEAD)
    text_kv = text_kv.reshape(text_total, local_heads, 2, HEAD)
    keys_all = jnp.concatenate([image_qkv[:, :, 1], text_kv[:, :, 0]], axis=0)
    values_all = jnp.concatenate([image_qkv[:, :, 2], text_kv[:, :, 1]], axis=0)
    slots = jnp.arange(text_total, dtype=jnp.int32)
    valid = jnp.concatenate([jnp.ones((image_total,), dtype=bool), slots < text_lengths[0, 0]])
    block_rows = local_rows
    while block_rows < 512 and image_total % (block_rows * 2) == 0:
        block_rows = block_rows * 2
    block_total = image_total // block_rows
    query_blocks = image_qkv[:, :, 0].reshape(block_total, block_rows, local_heads, HEAD)

    def attend(query_block):
        scores = jnp.einsum(
            "qhe,khe->hqk", query_block, keys_all, preferred_element_type=jnp.float32
        ) * HEAD ** (-0.5)
        scores = jnp.where(valid[None, None, :], scores, -1e30)
        row_max = jnp.max(scores, axis=2, keepdims=True)
        weights = jnp.exp(scores - row_max)
        total = jnp.sum(weights, axis=2, keepdims=True)
        probs = weights.astype(jnp.bfloat16)
        mixed = (
            jnp.einsum("hqk,khe->hqe", probs, values_all, preferred_element_type=jnp.float32)
            / total
        )
        return jnp.transpose(mixed.astype(jnp.bfloat16), (1, 0, 2))

    attended = lax.map(attend, query_blocks).reshape(image_total, local_heads * HEAD)
    attended = lax.all_to_all(attended, "seq", split_axis=0, concat_axis=1, tiled=True)
    hidden = image_rows.astype(jnp.float32) + mod_rows[2] * jnp.dot(
        attended, proj_weight, preferred_element_type=jnp.float32
    )
    mlp_norm = modulate(hidden, mod_rows[8], mod_rows[7])
    mlp_all = lax.all_gather(mlp_norm, "seq", axis=0, tiled=True)
    inner = jax.nn.gelu(
        jnp.dot(mlp_all, mlp_in_weight, preferred_element_type=jnp.float32), approximate=True
    ).astype(jnp.bfloat16)
    mlp_out = lax.psum_scatter(
        jnp.dot(inner, mlp_out_weight, preferred_element_type=jnp.float32).astype(jnp.bfloat16),
        "seq",
        scatter_dimension=0,
        tiled=True,
    ).astype(jnp.float32)
    block_out = hidden + mod_rows[9] * mlp_out
    final_norm = modulate(block_out, mod_rows[6], mod_rows[5])
    own_vel = lax.dot_general(
        final_weight, final_norm, (((1,), (1,)), ((), ())), preferred_element_type=jnp.float32
    )
    partner_vel = partner(own_vel.astype(jnp.bfloat16), "cfg", 0).astype(own_vel.dtype)
    leading = lax.axis_index("cfg") == 0
    cond_vel = jnp.where(leading, own_vel, partner_vel)
    uncond_vel = jnp.where(leading, partner_vel, own_vel)
    guided = uncond_vel + guidance[0] * (cond_vel - uncond_vel)
    cond_sq, guided_sq = lax.psum((jnp.sum(cond_vel * cond_vel), jnp.sum(guided * guided)), "seq")
    entries = own_vel.shape[0] * image_total
    rms_cond = jnp.sqrt(cond_sq / entries + EPS_NORM)
    rms_guided = jnp.sqrt(guided_sq / entries + EPS_NORM)
    result_vel = 0.7 * (guided * (rms_cond / rms_guided)) + 0.3 * guided
    channel_half = latents.shape[1]
    channel_start = lax.axis_index("cfg") * channel_half
    own_channels = lax.dynamic_slice_in_dim(result_vel, channel_start, channel_half, 0)
    next_index = jnp.minimum(step_index[0] + step_count[0], STEPS)
    step_size = sigma_of(next_index) - sigma_of(step_index[0])
    moved = latents[0] + step_size * own_channels
    return (own_channels[None], moved[None])


def solution(mesh):
    in_specs = (
        P("cfg", "req", "seq", None),
        P("cfg", "req", "seq", None),
        P("cfg", "req", None, None),
        P(None, "seq"),
        P(),
        P(None, "seq"),
        P("seq", None),
        P(),
        P("req", "cfg", "seq"),
        P("req"),
        P("cfg", "req"),
        P("req"),
        P("req"),
    )
    out_specs = (P("req", "cfg", "seq"), P("req", "cfg", "seq"))
    return jax.shard_map(local, mesh=mesh, in_specs=in_specs, out_specs=out_specs, check_vma=False)
```

```python
import jax
import jax.numpy as jnp
from jax import lax
from jax.sharding import PartitionSpec as P

HEADS = 16
HEAD = 64
STEPS = 28


EPS_NORM = 1e-06


def partner(value, axis, distance):
    mask = 2**distance
    pairs = [(source, source ^ mask) for source in range(lax.axis_size(axis))]
    return lax.ppermute(value, axis, pairs)


def shifted(value, axis, shift):
    size = lax.axis_size(axis)
    return lax.ppermute(value, axis, [(source, (source - shift) % size) for source in range(size)])


def modulate(rows_in, scale_row, shift_row):
    values = rows_in.astype(jnp.float32)
    center = jnp.mean(values, axis=-1, keepdims=True)
    spread = jnp.mean(jnp.square(values - center), axis=-1, keepdims=True)
    return (
        (values - center) * lax.rsqrt(spread + EPS_NORM) * (1.0 + scale_row) + shift_row
    ).astype(jnp.bfloat16)


def sigma_of(index):
    remain = 1.0 - index.astype(jnp.float32) / STEPS
    return 3.0 * remain / (1.0 + 2.0 * remain)


def split_columns(weight_piece):
    width_in = weight_piece.shape[0]
    head_count = weight_piece.shape[1] // (5 * HEAD)
    shaped = weight_piece.reshape(width_in, head_count, 5, HEAD)
    image_cols = shaped[:, :, 0:3, :].reshape(width_in, head_count * 3 * HEAD)
    text_cols = shaped[:, :, 3:5, :].reshape(width_in, head_count * 2 * HEAD)
    return (image_cols, text_cols)


def local(
    image_hidden,
    text_hidden,
    modulation,
    attn_weight,
    proj_weight,
    mlp_in_weight,
    mlp_out_weight,
    final_weight,
    latents,
    guidance,
    text_lengths,
    step_index,
    step_count,
):
    seq_size = lax.axis_size("seq")
    local_heads = HEADS // seq_size
    image_rows = image_hidden[0, 0]
    text_rows = text_hidden[0, 0]
    mod_rows = modulation[0, 0]
    local_rows = image_rows.shape[0]
    image_total = local_rows * seq_size
    text_total = text_rows.shape[0] * seq_size
    image_norm = modulate(image_rows, mod_rows[1], mod_rows[0])
    text_norm = modulate(text_rows, mod_rows[4], mod_rows[3])
    seq_index = lax.axis_index("seq")
    own_norm = jnp.concatenate([image_norm, text_norm], axis=0)
    gathered = jnp.stack([own_norm] + [shifted(own_norm, "seq", k) for k in range(1, seq_size)])
    image_all = gathered[:, :local_rows].reshape(image_total, -1)
    text_all = gathered[:, local_rows:].reshape(text_total, -1)
    image_cols, text_cols = split_columns(attn_weight)
    image_qkv = jnp.dot(image_all, image_cols, preferred_element_type=jnp.float32).astype(
        jnp.bfloat16
    )
    text_kv = jnp.dot(text_all, text_cols, preferred_element_type=jnp.float32).astype(
        jnp.bfloat16
    )
    image_qkv = image_qkv.reshape(image_total, local_heads, 3, HEAD)
    text_kv = text_kv.reshape(text_total, local_heads, 2, HEAD)
    keys_all = jnp.concatenate([image_qkv[:, :, 1], text_kv[:, :, 0]], axis=0)
    values_all = jnp.concatenate([image_qkv[:, :, 2], text_kv[:, :, 1]], axis=0)
    text_local = text_rows.shape[0]
    sources = (seq_index + jnp.arange(seq_size, dtype=jnp.int32)) % seq_size
    slots = (sources[:, None] * text_local + jnp.arange(text_local, dtype=jnp.int32)).reshape(-1)
    valid = jnp.concatenate([jnp.ones((image_total,), dtype=bool), slots < text_lengths[0, 0]])
    block_rows = local_rows
    while block_rows < 512 and image_total % (block_rows * 2) == 0:
        block_rows = block_rows * 2
    block_total = image_total // block_rows
    query_blocks = image_qkv[:, :, 0].reshape(block_total, block_rows, local_heads, HEAD)

    def attend(query_block):
        scores = jnp.einsum(
            "qhe,khe->hqk", query_block, keys_all, preferred_element_type=jnp.float32
        ) * HEAD ** (-0.5)
        scores = jnp.where(valid[None, None, :], scores, -1e30)
        row_max = jnp.max(scores, axis=2, keepdims=True)
        weights = jnp.exp(scores - row_max)
        total = jnp.sum(weights, axis=2, keepdims=True)
        probs = weights.astype(jnp.bfloat16)
        mixed = (
            jnp.einsum("hqk,khe->hqe", probs, values_all, preferred_element_type=jnp.float32)
            / total
        )
        return jnp.transpose(mixed.astype(jnp.bfloat16), (1, 0, 2))

    attended = lax.map(attend, query_blocks).reshape(image_total, local_heads * HEAD)
    attended = attended.reshape(seq_size, local_rows, local_heads * HEAD)
    head_width = local_heads * HEAD
    projected = jnp.zeros((local_rows, proj_weight.shape[1]), jnp.float32)
    for k in range(seq_size):
        piece = attended[k] if k == 0 else shifted(attended[k], "seq", -k)
        rows = lax.dynamic_slice_in_dim(
            proj_weight, ((seq_index - k) % seq_size) * head_width, head_width, 0
        )
        projected = projected + jnp.dot(piece, rows, preferred_element_type=jnp.float32)
    hidden = image_rows.astype(jnp.float32) + mod_rows[2] * projected
    mlp_norm = modulate(hidden, mod_rows[8], mod_rows[7])
    mlp_out = jnp.zeros((local_rows, mlp_out_weight.shape[1]), jnp.float32)
    for k in range(seq_size):
        piece = mlp_norm if k == 0 else shifted(mlp_norm, "seq", k)
        inner = jax.nn.gelu(
            jnp.dot(piece, mlp_in_weight, preferred_element_type=jnp.float32), approximate=True
        ).astype(jnp.bfloat16)
        part = jnp.dot(inner, mlp_out_weight, preferred_element_type=jnp.float32).astype(
            jnp.bfloat16
        )
        part = part if k == 0 else shifted(part, "seq", -k)
        mlp_out = mlp_out + part.astype(jnp.float32)
    block_out = hidden + mod_rows[9] * mlp_out
    final_norm = modulate(block_out, mod_rows[6], mod_rows[5])
    own_vel = lax.dot_general(
        final_weight, final_norm, (((1,), (1,)), ((), ())), preferred_element_type=jnp.float32
    )
    partner_vel = partner(own_vel.astype(jnp.bfloat16), "cfg", 0).astype(own_vel.dtype)
    leading = lax.axis_index("cfg") == 0
    cond_vel = jnp.where(leading, own_vel, partner_vel)
    uncond_vel = jnp.where(leading, partner_vel, own_vel)
    guided = uncond_vel + guidance[0] * (cond_vel - uncond_vel)
    squares = jnp.stack([jnp.sum(cond_vel * cond_vel), jnp.sum(guided * guided)])
    for bit in range(seq_size.bit_length() - 1):
        squares = squares + partner(squares, "seq", bit)
    cond_sq, guided_sq = squares[0], squares[1]
    entries = own_vel.shape[0] * image_total
    rms_cond = jnp.sqrt(cond_sq / entries + EPS_NORM)
    rms_guided = jnp.sqrt(guided_sq / entries + EPS_NORM)
    result_vel = 0.7 * (guided * (rms_cond / rms_guided)) + 0.3 * guided
    channel_half = latents.shape[1]
    channel_start = lax.axis_index("cfg") * channel_half
    own_channels = lax.dynamic_slice_in_dim(result_vel, channel_start, channel_half, 0)
    next_index = jnp.minimum(step_index[0] + step_count[0], STEPS)
    step_size = sigma_of(next_index) - sigma_of(step_index[0])
    moved = latents[0] + step_size * own_channels
    return (own_channels[None], moved[None])


def solution(mesh):
    in_specs = (
        P("cfg", "req", "seq", None),
        P("cfg", "req", "seq", None),
        P("cfg", "req", None, None),
        P(None, "seq"),
        P(),
        P(None, "seq"),
        P("seq", None),
        P(),
        P("req", "cfg", "seq"),
        P("req"),
        P("cfg", "req"),
        P("req"),
        P("req"),
    )
    out_specs = (P("req", "cfg", "seq"), P("req", "cfg", "seq"))
    return jax.shard_map(local, mesh=mesh, in_specs=in_specs, out_specs=out_specs, check_vma=False)
```

```python
import jax
import jax.numpy as jnp
from jax import lax
from jax.sharding import PartitionSpec as P

HEADS = 16
HEAD = 64
STEPS = 28


EPS_NORM = 1e-06


def partner(value, axis, distance):
    mask = 2**distance
    pairs = [(source, source ^ mask) for source in range(lax.axis_size(axis))]
    return lax.ppermute(value, axis, pairs)


def shifted(value, axis, shift):
    size = lax.axis_size(axis)
    return lax.ppermute(value, axis, [(source, (source - shift) % size) for source in range(size)])


def modulate(rows_in, scale_row, shift_row):
    values = rows_in.astype(jnp.float32)
    center = jnp.mean(values, axis=-1, keepdims=True)
    spread = jnp.mean(jnp.square(values - center), axis=-1, keepdims=True)
    return (
        (values - center) * lax.rsqrt(spread + EPS_NORM) * (1.0 + scale_row) + shift_row
    ).astype(jnp.bfloat16)


def sigma_of(index):
    remain = 1.0 - index.astype(jnp.float32) / STEPS
    return 3.0 * remain / (1.0 + 2.0 * remain)


def split_columns(weight_piece):
    width_in = weight_piece.shape[0]
    head_count = weight_piece.shape[1] // (5 * HEAD)
    shaped = weight_piece.reshape(width_in, head_count, 5, HEAD)
    image_cols = shaped[:, :, 0:3, :].reshape(width_in, head_count * 3 * HEAD)
    text_cols = shaped[:, :, 3:5, :].reshape(width_in, head_count * 2 * HEAD)
    return (image_cols, text_cols)


def local(
    image_hidden,
    text_hidden,
    modulation,
    attn_weight,
    proj_weight,
    mlp_in_weight,
    mlp_out_weight,
    final_weight,
    latents,
    guidance,
    text_lengths,
    step_index,
    step_count,
):
    seq_size = lax.axis_size("seq")
    local_heads = HEADS // seq_size
    image_rows = image_hidden[0, 0]
    text_rows = text_hidden[0, 0]
    mod_rows = modulation[0, 0]
    local_rows = image_rows.shape[0]
    image_total = local_rows * seq_size
    text_total = text_rows.shape[0] * seq_size
    image_norm = modulate(image_rows, mod_rows[1], mod_rows[0])
    text_norm = modulate(text_rows, mod_rows[4], mod_rows[3])
    gathered = lax.all_gather(jnp.concatenate([image_norm, text_norm], axis=0), "seq", axis=0)
    image_all = gathered[:, :local_rows].reshape(image_total, -1)
    text_all = gathered[:, local_rows:].reshape(text_total, -1)
    image_cols, text_cols = split_columns(attn_weight)
    image_qkv = jnp.dot(image_all, image_cols, preferred_element_type=jnp.float32).astype(
        jnp.bfloat16
    )
    text_kv = jnp.dot(text_all, text_cols, preferred_element_type=jnp.float32).astype(
        jnp.bfloat16
    )
    image_qkv = image_qkv.reshape(image_total, local_heads, 3, HEAD)
    text_kv = text_kv.reshape(text_total, local_heads, 2, HEAD)
    keys_all = jnp.concatenate([image_qkv[:, :, 1], text_kv[:, :, 0]], axis=0)
    values_all = jnp.concatenate([image_qkv[:, :, 2], text_kv[:, :, 1]], axis=0)
    slots = jnp.arange(text_total, dtype=jnp.int32)
    valid = jnp.concatenate([jnp.ones((image_total,), dtype=bool), slots < text_lengths[0, 0]])
    block_rows = local_rows
    while block_rows < 512 and image_total % (block_rows * 2) == 0:
        block_rows = block_rows * 2
    block_total = image_total // block_rows
    query_blocks = image_qkv[:, :, 0].reshape(block_total, block_rows, local_heads, HEAD)

    def attend(query_block):
        scores = jnp.einsum(
            "qhe,khe->hqk", query_block, keys_all, preferred_element_type=jnp.float32
        ) * HEAD ** (-0.5)
        scores = jnp.where(valid[None, None, :], scores, -1e30)
        row_max = jnp.max(scores, axis=2, keepdims=True)
        weights = jnp.exp(scores - row_max)
        total = jnp.sum(weights, axis=2, keepdims=True)
        probs = weights.astype(jnp.bfloat16)
        mixed = (
            jnp.einsum("hqk,khe->hqe", probs, values_all, preferred_element_type=jnp.float32)
            / total
        )
        return jnp.transpose(mixed.astype(jnp.bfloat16), (1, 0, 2))

    attended = lax.map(attend, query_blocks).reshape(image_total, local_heads * HEAD)
    attended = lax.all_to_all(attended, "seq", split_axis=0, concat_axis=1, tiled=True)
    hidden = image_rows.astype(jnp.float32) + mod_rows[2] * jnp.dot(
        attended, proj_weight, preferred_element_type=jnp.float32
    )
    mlp_norm = modulate(hidden, mod_rows[8], mod_rows[7])
    mlp_out = jnp.zeros((local_rows, mlp_out_weight.shape[1]), jnp.float32)
    for k in range(seq_size):
        piece = mlp_norm if k == 0 else shifted(mlp_norm, "seq", k)
        inner = jax.nn.gelu(
            jnp.dot(piece, mlp_in_weight, preferred_element_type=jnp.float32), approximate=True
        ).astype(jnp.bfloat16)
        part = jnp.dot(inner, mlp_out_weight, preferred_element_type=jnp.float32).astype(
            jnp.bfloat16
        )
        part = part if k == 0 else shifted(part, "seq", -k)
        mlp_out = mlp_out + part.astype(jnp.float32)
    block_out = hidden + mod_rows[9] * mlp_out
    final_norm = modulate(block_out, mod_rows[6], mod_rows[5])
    own_vel = lax.dot_general(
        final_weight, final_norm, (((1,), (1,)), ((), ())), preferred_element_type=jnp.float32
    )
    partner_vel = partner(own_vel.astype(jnp.bfloat16), "cfg", 0).astype(own_vel.dtype)
    leading = lax.axis_index("cfg") == 0
    cond_vel = jnp.where(leading, own_vel, partner_vel)
    uncond_vel = jnp.where(leading, partner_vel, own_vel)
    guided = uncond_vel + guidance[0] * (cond_vel - uncond_vel)
    squares = jnp.stack([jnp.sum(cond_vel * cond_vel), jnp.sum(guided * guided)])
    for bit in range(seq_size.bit_length() - 1):
        squares = squares + partner(squares, "seq", bit)
    cond_sq, guided_sq = squares[0], squares[1]
    entries = own_vel.shape[0] * image_total
    rms_cond = jnp.sqrt(cond_sq / entries + EPS_NORM)
    rms_guided = jnp.sqrt(guided_sq / entries + EPS_NORM)
    result_vel = 0.7 * (guided * (rms_cond / rms_guided)) + 0.3 * guided
    channel_half = latents.shape[1]
    channel_start = lax.axis_index("cfg") * channel_half
    own_channels = lax.dynamic_slice_in_dim(result_vel, channel_start, channel_half, 0)
    next_index = jnp.minimum(step_index[0] + step_count[0], STEPS)
    step_size = sigma_of(next_index) - sigma_of(step_index[0])
    moved = latents[0] + step_size * own_channels
    return (own_channels[None], moved[None])


def solution(mesh):
    in_specs = (
        P("cfg", "req", "seq", None),
        P("cfg", "req", "seq", None),
        P("cfg", "req", None, None),
        P(None, "seq"),
        P(),
        P(None, "seq"),
        P("seq", None),
        P(),
        P("req", "cfg", "seq"),
        P("req"),
        P("cfg", "req"),
        P("req"),
        P("req"),
    )
    out_specs = (P("req", "cfg", "seq"), P("req", "cfg", "seq"))
    return jax.shard_map(local, mesh=mesh, in_specs=in_specs, out_specs=out_specs, check_vma=False)
```

```python
import jax
import jax.numpy as jnp
from jax import lax
from jax.sharding import PartitionSpec as P

HEADS = 16
HEAD = 64
STEPS = 28


EPS_NORM = 1e-06


def partner(value, axis, distance):
    mask = 2**distance
    pairs = [(source, source ^ mask) for source in range(lax.axis_size(axis))]
    return lax.ppermute(value, axis, pairs)


def shifted(value, axis, shift):
    size = lax.axis_size(axis)
    return lax.ppermute(value, axis, [(source, (source - shift) % size) for source in range(size)])


def modulate(rows_in, scale_row, shift_row):
    values = rows_in.astype(jnp.float32)
    center = jnp.mean(values, axis=-1, keepdims=True)
    spread = jnp.mean(jnp.square(values - center), axis=-1, keepdims=True)
    return (
        (values - center) * lax.rsqrt(spread + EPS_NORM) * (1.0 + scale_row) + shift_row
    ).astype(jnp.bfloat16)


def sigma_of(index):
    remain = 1.0 - index.astype(jnp.float32) / STEPS
    return 3.0 * remain / (1.0 + 2.0 * remain)


def split_columns(weight_piece):
    width_in = weight_piece.shape[0]
    head_count = weight_piece.shape[1] // (5 * HEAD)
    shaped = weight_piece.reshape(width_in, head_count, 5, HEAD)
    image_cols = shaped[:, :, 0:3, :].reshape(width_in, head_count * 3 * HEAD)
    text_cols = shaped[:, :, 3:5, :].reshape(width_in, head_count * 2 * HEAD)
    return (image_cols, text_cols)


def local(
    image_hidden,
    text_hidden,
    modulation,
    attn_weight,
    proj_weight,
    mlp_in_weight,
    mlp_out_weight,
    final_weight,
    latents,
    guidance,
    text_lengths,
    step_index,
    step_count,
):
    seq_size = lax.axis_size("seq")
    local_heads = HEADS // seq_size
    image_rows = image_hidden[0, 0]
    text_rows = text_hidden[0, 0]
    mod_rows = modulation[0, 0]
    local_rows = image_rows.shape[0]
    image_total = local_rows * seq_size
    text_total = text_rows.shape[0] * seq_size
    image_norm = modulate(image_rows, mod_rows[1], mod_rows[0])
    text_norm = modulate(text_rows, mod_rows[4], mod_rows[3])
    seq_index = lax.axis_index("seq")
    own_norm = jnp.concatenate([image_norm, text_norm], axis=0)
    image_cols, text_cols = split_columns(attn_weight)
    image_parts = []
    text_parts = []
    for k in range(seq_size):
        piece = own_norm if k == 0 else shifted(own_norm, "seq", k)
        image_parts.append(
            jnp.dot(piece[:local_rows], image_cols, preferred_element_type=jnp.float32).astype(
                jnp.bfloat16
            )
        )
        text_parts.append(
            jnp.dot(piece[local_rows:], text_cols, preferred_element_type=jnp.float32).astype(
                jnp.bfloat16
            )
        )
    image_qkv = jnp.concatenate(image_parts, axis=0)
    text_kv = jnp.concatenate(text_parts, axis=0)
    image_qkv = image_qkv.reshape(image_total, local_heads, 3, HEAD)
    text_kv = text_kv.reshape(text_total, local_heads, 2, HEAD)
    keys_all = jnp.concatenate([image_qkv[:, :, 1], text_kv[:, :, 0]], axis=0)
    values_all = jnp.concatenate([image_qkv[:, :, 2], text_kv[:, :, 1]], axis=0)
    text_local = text_rows.shape[0]
    sources = (seq_index + jnp.arange(seq_size, dtype=jnp.int32)) % seq_size
    slots = (sources[:, None] * text_local + jnp.arange(text_local, dtype=jnp.int32)).reshape(-1)
    valid = jnp.concatenate([jnp.ones((image_total,), dtype=bool), slots < text_lengths[0, 0]])
    block_rows = local_rows
    while block_rows < 512 and image_total % (block_rows * 2) == 0:
        block_rows = block_rows * 2
    block_total = image_total // block_rows
    query_blocks = image_qkv[:, :, 0].reshape(block_total, block_rows, local_heads, HEAD)

    def attend(query_block):
        scores = jnp.einsum(
            "qhe,khe->hqk", query_block, keys_all, preferred_element_type=jnp.float32
        ) * HEAD ** (-0.5)
        scores = jnp.where(valid[None, None, :], scores, -1e30)
        row_max = jnp.max(scores, axis=2, keepdims=True)
        weights = jnp.exp(scores - row_max)
        total = jnp.sum(weights, axis=2, keepdims=True)
        probs = weights.astype(jnp.bfloat16)
        mixed = (
            jnp.einsum("hqk,khe->hqe", probs, values_all, preferred_element_type=jnp.float32)
            / total
        )
        return jnp.transpose(mixed.astype(jnp.bfloat16), (1, 0, 2))

    attended = lax.map(attend, query_blocks).reshape(image_total, local_heads * HEAD)
    attended = attended.reshape(seq_size, local_rows, local_heads * HEAD)
    head_width = local_heads * HEAD
    projected = jnp.zeros((local_rows, proj_weight.shape[1]), jnp.float32)
    for k in range(seq_size):
        piece = attended[k] if k == 0 else shifted(attended[k], "seq", -k)
        rows = lax.dynamic_slice_in_dim(
            proj_weight, ((seq_index - k) % seq_size) * head_width, head_width, 0
        )
        projected = projected + jnp.dot(piece, rows, preferred_element_type=jnp.float32)
    hidden = image_rows.astype(jnp.float32) + mod_rows[2] * projected
    mlp_norm = modulate(hidden, mod_rows[8], mod_rows[7])
    mlp_out = jnp.zeros((local_rows, mlp_out_weight.shape[1]), jnp.float32)
    for k in range(seq_size):
        piece = mlp_norm if k == 0 else shifted(mlp_norm, "seq", k)
        inner = jax.nn.gelu(
            jnp.dot(piece, mlp_in_weight, preferred_element_type=jnp.float32), approximate=True
        ).astype(jnp.bfloat16)
        part = jnp.dot(inner, mlp_out_weight, preferred_element_type=jnp.float32).astype(
            jnp.bfloat16
        )
        part = part if k == 0 else shifted(part, "seq", -k)
        mlp_out = mlp_out + part.astype(jnp.float32)
    block_out = hidden + mod_rows[9] * mlp_out
    final_norm = modulate(block_out, mod_rows[6], mod_rows[5])
    own_vel = lax.dot_general(
        final_weight, final_norm, (((1,), (1,)), ((), ())), preferred_element_type=jnp.float32
    )
    partner_vel = partner(own_vel.astype(jnp.bfloat16), "cfg", 0).astype(own_vel.dtype)
    leading = lax.axis_index("cfg") == 0
    cond_vel = jnp.where(leading, own_vel, partner_vel)
    uncond_vel = jnp.where(leading, partner_vel, own_vel)
    guided = uncond_vel + guidance[0] * (cond_vel - uncond_vel)
    squares = jnp.stack([jnp.sum(cond_vel * cond_vel), jnp.sum(guided * guided)])
    for bit in range(seq_size.bit_length() - 1):
        squares = squares + partner(squares, "seq", bit)
    cond_sq, guided_sq = squares[0], squares[1]
    entries = own_vel.shape[0] * image_total
    rms_cond = jnp.sqrt(cond_sq / entries + EPS_NORM)
    rms_guided = jnp.sqrt(guided_sq / entries + EPS_NORM)
    result_vel = 0.7 * (guided * (rms_cond / rms_guided)) + 0.3 * guided
    channel_half = latents.shape[1]
    channel_start = lax.axis_index("cfg") * channel_half
    own_channels = lax.dynamic_slice_in_dim(result_vel, channel_start, channel_half, 0)
    next_index = jnp.minimum(step_index[0] + step_count[0], STEPS)
    step_size = sigma_of(next_index) - sigma_of(step_index[0])
    moved = latents[0] + step_size * own_channels
    return (own_channels[None], moved[None])


def solution(mesh):
    in_specs = (
        P("cfg", "req", "seq", None),
        P("cfg", "req", "seq", None),
        P("cfg", "req", None, None),
        P(None, "seq"),
        P(),
        P(None, "seq"),
        P("seq", None),
        P(),
        P("req", "cfg", "seq"),
        P("req"),
        P("cfg", "req"),
        P("req"),
        P("req"),
    )
    out_specs = (P("req", "cfg", "seq"), P("req", "cfg", "seq"))
    return jax.shard_map(local, mesh=mesh, in_specs=in_specs, out_specs=out_specs, check_vma=False)
```

```python
import jax
import jax.numpy as jnp
from jax import lax
from jax.sharding import PartitionSpec as P

HEADS = 16
HEAD = 64
STEPS = 28


EPS_NORM = 1e-06


def partner(value, axis, distance):
    mask = 2**distance
    pairs = [(source, source ^ mask) for source in range(lax.axis_size(axis))]
    return lax.ppermute(value, axis, pairs)


def shifted(value, axis, shift):
    size = lax.axis_size(axis)
    return lax.ppermute(value, axis, [(source, (source - shift) % size) for source in range(size)])


def modulate(rows_in, scale_row, shift_row):
    values = rows_in.astype(jnp.float32)
    center = jnp.mean(values, axis=-1, keepdims=True)
    spread = jnp.mean(jnp.square(values - center), axis=-1, keepdims=True)
    return (
        (values - center) * lax.rsqrt(spread + EPS_NORM) * (1.0 + scale_row) + shift_row
    ).astype(jnp.bfloat16)


def sigma_of(index):
    remain = 1.0 - index.astype(jnp.float32) / STEPS
    return 3.0 * remain / (1.0 + 2.0 * remain)


def split_columns(weight_piece):
    width_in = weight_piece.shape[0]
    head_count = weight_piece.shape[1] // (5 * HEAD)
    shaped = weight_piece.reshape(width_in, head_count, 5, HEAD)
    image_cols = shaped[:, :, 0:3, :].reshape(width_in, head_count * 3 * HEAD)
    text_cols = shaped[:, :, 3:5, :].reshape(width_in, head_count * 2 * HEAD)
    return (image_cols, text_cols)


def local(
    image_hidden,
    text_hidden,
    modulation,
    attn_weight,
    proj_weight,
    mlp_in_weight,
    mlp_out_weight,
    final_weight,
    latents,
    guidance,
    text_lengths,
    step_index,
    step_count,
):
    seq_size = lax.axis_size("seq")
    local_heads = HEADS // seq_size
    image_rows = image_hidden[0, 0]
    text_rows = text_hidden[0, 0]
    mod_rows = modulation[0, 0]
    local_rows = image_rows.shape[0]
    image_total = local_rows * seq_size
    text_total = text_rows.shape[0] * seq_size
    image_norm = modulate(image_rows, mod_rows[1], mod_rows[0])
    text_norm = modulate(text_rows, mod_rows[4], mod_rows[3])
    seq_index = lax.axis_index("seq")
    own_norm = jnp.concatenate([image_norm, text_norm], axis=0)
    gathered = jnp.stack([own_norm] + [shifted(own_norm, "seq", k) for k in range(1, seq_size)])
    image_all = gathered[:, :local_rows].reshape(image_total, -1)
    text_all = gathered[:, local_rows:].reshape(text_total, -1)
    image_cols, text_cols = split_columns(attn_weight)
    image_qkv = jnp.dot(image_all, image_cols, preferred_element_type=jnp.float32).astype(
        jnp.bfloat16
    )
    text_kv = jnp.dot(text_all, text_cols, preferred_element_type=jnp.float32).astype(
        jnp.bfloat16
    )
    image_qkv = image_qkv.reshape(image_total, local_heads, 3, HEAD)
    text_kv = text_kv.reshape(text_total, local_heads, 2, HEAD)
    keys_all = jnp.concatenate([image_qkv[:, :, 1], text_kv[:, :, 0]], axis=0)
    values_all = jnp.concatenate([image_qkv[:, :, 2], text_kv[:, :, 1]], axis=0)
    text_local = text_rows.shape[0]
    sources = (seq_index + jnp.arange(seq_size, dtype=jnp.int32)) % seq_size
    slots = (sources[:, None] * text_local + jnp.arange(text_local, dtype=jnp.int32)).reshape(-1)
    valid = jnp.concatenate([jnp.ones((image_total,), dtype=bool), slots < text_lengths[0, 0]])
    block_rows = local_rows
    while block_rows < 512 and image_total % (block_rows * 2) == 0:
        block_rows = block_rows * 2
    block_total = image_total // block_rows
    query_blocks = image_qkv[:, :, 0].reshape(block_total, block_rows, local_heads, HEAD)

    def attend(query_block):
        scores = jnp.einsum(
            "qhe,khe->hqk", query_block, keys_all, preferred_element_type=jnp.float32
        ) * HEAD ** (-0.5)
        scores = jnp.where(valid[None, None, :], scores, -1e30)
        row_max = jnp.max(scores, axis=2, keepdims=True)
        weights = jnp.exp(scores - row_max)
        total = jnp.sum(weights, axis=2, keepdims=True)
        probs = weights.astype(jnp.bfloat16)
        mixed = (
            jnp.einsum("hqk,khe->hqe", probs, values_all, preferred_element_type=jnp.float32)
            / total
        )
        return jnp.transpose(mixed.astype(jnp.bfloat16), (1, 0, 2))

    attended = lax.map(attend, query_blocks).reshape(image_total, local_heads * HEAD)
    attended = attended.reshape(seq_size, local_rows, local_heads * HEAD)
    head_width = local_heads * HEAD
    projected = jnp.zeros((local_rows, proj_weight.shape[1]), jnp.float32)
    for k in range(seq_size):
        piece = attended[k] if k == 0 else shifted(attended[k], "seq", -k)
        rows = lax.dynamic_slice_in_dim(
            proj_weight, ((seq_index - k) % seq_size) * head_width, head_width, 0
        )
        projected = projected + jnp.dot(piece, rows, preferred_element_type=jnp.float32)
    hidden = image_rows.astype(jnp.float32) + mod_rows[2] * projected
    mlp_norm = modulate(hidden, mod_rows[8], mod_rows[7])
    mlp_out = jnp.zeros((local_rows, mlp_out_weight.shape[1]), jnp.float32)
    for k in range(seq_size):
        piece = mlp_norm if k == 0 else shifted(mlp_norm, "seq", k)
        inner = jax.nn.gelu(
            jnp.dot(piece, mlp_in_weight, preferred_element_type=jnp.float32), approximate=True
        ).astype(jnp.bfloat16)
        part = jnp.dot(inner, mlp_out_weight, preferred_element_type=jnp.float32).astype(
            jnp.bfloat16
        )
        part = part if k == 0 else shifted(part, "seq", -k)
        mlp_out = mlp_out + part.astype(jnp.float32)
    block_out = hidden + mod_rows[9] * mlp_out
    final_norm = modulate(block_out, mod_rows[6], mod_rows[5])
    own_vel = lax.dot_general(
        final_weight, final_norm, (((1,), (1,)), ((), ())), preferred_element_type=jnp.float32
    )
    partner_vel = partner(own_vel.astype(jnp.bfloat16), "cfg", 0).astype(own_vel.dtype)
    leading = lax.axis_index("cfg") == 0
    cond_vel = jnp.where(leading, own_vel, partner_vel)
    uncond_vel = jnp.where(leading, partner_vel, own_vel)
    guided = uncond_vel + guidance[0] * (cond_vel - uncond_vel)
    squares = jnp.stack([jnp.sum(cond_vel * cond_vel), jnp.sum(guided * guided)])
    squares = sum(
        [squares] + [shifted(squares, "seq", k) for k in range(1, seq_size)], jnp.zeros(2)
    )
    cond_sq, guided_sq = squares[0], squares[1]
    entries = own_vel.shape[0] * image_total
    rms_cond = jnp.sqrt(cond_sq / entries + EPS_NORM)
    rms_guided = jnp.sqrt(guided_sq / entries + EPS_NORM)
    result_vel = 0.7 * (guided * (rms_cond / rms_guided)) + 0.3 * guided
    channel_half = latents.shape[1]
    channel_start = lax.axis_index("cfg") * channel_half
    own_channels = lax.dynamic_slice_in_dim(result_vel, channel_start, channel_half, 0)
    next_index = jnp.minimum(step_index[0] + step_count[0], STEPS)
    step_size = sigma_of(next_index) - sigma_of(step_index[0])
    moved = latents[0] + step_size * own_channels
    return (own_channels[None], moved[None])


def solution(mesh):
    in_specs = (
        P("cfg", "req", "seq", None),
        P("cfg", "req", "seq", None),
        P("cfg", "req", None, None),
        P(None, "seq"),
        P(),
        P(None, "seq"),
        P("seq", None),
        P(),
        P("req", "cfg", "seq"),
        P("req"),
        P("cfg", "req"),
        P("req"),
        P("req"),
    )
    out_specs = (P("req", "cfg", "seq"), P("req", "cfg", "seq"))
    return jax.shard_map(local, mesh=mesh, in_specs=in_specs, out_specs=out_specs, check_vma=False)
```
